512 devices in a mesh: req: 128 (over y, z, core), tp: 4 (over x).
Axes of the slice: x: 4, y: 8, z: 8, core: 2. Of those that a mesh axis runs over, the one named last changes fastest.
Arguments:
- hidden: bfloat16 [1024, 4096], P('req'), may hold values from -512 to 512
- norm_gain: bfloat16 [4096], replicated, may hold values from 1 to 3
- lm_head: bfloat16 [4096, 131072], P(None, ('req', 'tp'))
- targets: int32 [1024], P('req'), may hold values from 0 to 131071
- segments: int32 [1024], P('req'), may hold values from 0 to 3, never falling along the last dimension, each value on 1 to 512 neighbouring positions
- scored: int32 [1024], P('req'), may hold values from 0 to 1, as said below
Outputs:
- token_logprob: float32 [1024], P('req')
- token_entropy: float32 [1024], P('req')
- seq_logprob: float32 [4], replicated
The draws below stay inside these ranges and needn't reach their ends.
Inputs may be any that keep to these rules, and one draw needn't show every extreme that they name: At most 4 of the 8 rows of one index of req are scored, and exactly 4 on some index in every draw.
All inputs are finite; a program needn't handle non-finite values.
Results may differ from the reference program's by a relative error of at most 0.0061.
Values may be sent and summed in bfloat16 or wider, within the bound.
A program may use at most 64 MiB of HBM per device.

```python
import math
import jax
import jax.numpy as jnp
import numpy as np
from jax import lax

D = 4096
VOCAB = 131072
TOK_REQ = 8
SCORE_MOST = 4
TOKENS = 1024
SEQS = 4


def head_block(key, block_index):
    return jax.random.normal(jax.random.fold_in(key, block_index), (D, 128), jnp.float32) * (3.0 / math.sqrt(D))


def drawn_plan(key):
    base = jax.random.fold_in(key, 11)
    keys = jax.random.split(jax.random.fold_in(key, 53), 5)
    count = min(16, TOKENS)
    pairs = jax.random.permutation(keys[0], VOCAB // 2)[:count].astype(jnp.int32)
    first_cols = pairs * 2
    ladder = jnp.exp(jnp.arange(count, dtype=jnp.float32) * (math.log(24.0) / max(count - 1, 1)))
    power = ladder[jax.random.permutation(keys[3], count)]
    factor = power * (9.5 / math.sqrt(D))

    def raw_column(column):
        block_data = head_block(base, column // 128)
        return lax.dynamic_slice_in_dim(block_data, column % 128, 1, 1)[:, 0]
    raw_cols = jax.vmap(raw_column)(first_cols)
    fresh = jax.random.normal(keys[1], (count, D), jnp.float32) * (0.5 * 3.0 / math.sqrt(D))
    first_new = raw_cols * factor[:, None]
    second_new = first_new + fresh
    positions = jax.random.permutation(keys[4], TOKENS)[:count].astype(jnp.int32)
    return (first_cols, raw_cols, first_new, second_new, keys[2], count, positions)


def draw_lm_head(key, part):
    base = jax.random.fold_in(key, 11)
    blocks = jax.vmap(lambda block_index: head_block(base, block_index))(jnp.arange(VOCAB // 128))
    whole = jnp.transpose(blocks, (1, 0, 2)).reshape(D, VOCAB)
    first_cols, raw_cols, first_new, second_new, unused_key, count, unused_rows = drawn_plan(key)
    whole = whole.at[:, first_cols].set(jnp.transpose(first_new))
    whole = whole.at[:, first_cols + 1].set(jnp.transpose(second_new))
    return whole.astype(jnp.bfloat16)


def draw_hidden(key, part):
    keys = jax.random.split(jax.random.fold_in(key, 23), 3)
    row_scale = jnp.exp(jax.random.uniform(keys[0], (TOKENS, 1)) * math.log(10.0))
    col_scale = jnp.exp(jax.random.uniform(keys[1], (1, D)) * math.log(10.0))
    values = jnp.clip(jax.random.normal(keys[2], (TOKENS, D)), -4.0, 4.0) * row_scale * col_scale
    first_cols, raw_cols, first_new, second_new, noise_key, count, positions = drawn_plan(key)
    new_rows = raw_cols * (math.sqrt(D) / 3.0) + 0.3 * jax.random.normal(noise_key, (count, D), jnp.float32)
    values = values.at[positions].set(new_rows)
    return jnp.clip(values, -512.0, 512.0).astype(jnp.bfloat16)


def draw_scored(key, part):
    keys = jax.random.split(jax.random.fold_in(key, 37), 3)
    groups = TOKENS // TOK_REQ
    counts = jax.random.randint(keys[0], (groups,), 1, SCORE_MOST + 1)
    fullest = jax.random.randint(keys[1], (), 0, groups)
    counts = jnp.where(jnp.arange(groups) == fullest, SCORE_MOST, counts)
    ranks = jax.vmap(lambda row_key: jax.random.permutation(row_key, TOK_REQ))(jax.random.split(keys[2], groups))
    return (ranks < counts[:, None]).astype(jnp.int32).reshape(TOKENS)


def plant(result, own_key, low, high):
    shape = result.shape
    index_at = [jax.random.randint(jax.random.fold_in(own_key, axis), (), 0, shape[axis]) for axis in range(len(shape))]
    result = result.at[tuple(index_at)].set(low)
    longest = shape.index(max(shape))
    index_at[longest] = (index_at[longest] + 1) % shape[longest]
    return result.at[tuple(index_at)].set(high)


def ranked_wide(key, dims, number_of, lean):
    loads = [min(1 << octave, number_of + 1 - (1 << octave)) * (1 << 20) // math.isqrt((1 << octave) ** lean) + 1 for octave in range((number_of + 1).bit_length()) if 1 << octave <= number_of]
    deviation = 1 + sum(loads) // (1 << 30)
    listing = np.cumsum(np.array([max(1, weight // deviation) for weight in loads]))
    lot = jax.random.randint(jax.random.fold_in(key, 1), dims, 0, int(listing[len(loads) - 1]))
    start = jnp.left_shift(1, jnp.searchsorted(jnp.asarray(listing, jnp.int32), lot, side="right").astype(jnp.int32))
    rank = start - 1 + jax.random.randint(jax.random.fold_in(key, 4), dims, 0, 1 << 30) % jnp.minimum(start, number_of + 1 - start)
    return jax.random.permutation(jax.random.fold_in(key, 2), number_of)[rank].astype(jnp.int32)


def length_profile(number_of, total, bound, slope):
    portions = [(1 << 20) // math.isqrt(standing ** slope) + 1 for standing in range(2, number_of + 1)]
    rest, given = total - bound - (number_of - 1), [1] * (number_of - 1)
    while rest > 0:
        movable = [i for i in range(number_of - 1) if given[i] < bound]
        whole, budget = sum([portions[i] for i in movable]), rest
        for i in movable:
            more = min(bound - given[i], max(1, budget * portions[i] // whole), rest)
            given[i] = given[i] + more
            rest = rest - more
    return np.array([bound] + given)


def ragged_sizes(key, number_of, total, reach, slope):
    if number_of == 2:
        one = jax.random.randint(key, (), max(1, total - reach), min(reach, total - 1) + 1)
        return jnp.stack([one, total - one])
    lengths = jnp.asarray(length_profile(number_of, total, reach, slope), jnp.int32)
    twos = (number_of - 1) // 2
    source_of, taker = lengths[1:1 + 2 * twos:2], lengths[2:2 + 2 * twos:2]
    margin = jnp.minimum(source_of - 1, reach - taker)
    moved = jax.random.randint(jax.random.fold_in(key, 1), (twos,), 0, 1 << 20) % (margin + 1)
    lengths = lengths.at[1:1 + 2 * twos:2].set(source_of - moved).at[2:2 + 2 * twos:2].set(taker + moved)
    return lengths[jax.random.permutation(jax.random.fold_in(key, 2), number_of)]


def setup_inputs(seed: int = 0) -> dict:
    seeds = jax.random.split(jax.random.key(seed), 7)
    hidden = draw_hidden(jax.random.fold_in(seeds[6], 71), 0)
    norm_gain = jnp.clip(jnp.exp(jax.random.uniform(seeds[1], (D,), jnp.float32, math.log(1.0), math.log(3.0))), 1.0, 3.0).astype(jnp.bfloat16)
    lm_head = draw_lm_head(jax.random.fold_in(seeds[6], 71), 0)
    targets = plant(ranked_wide(seeds[3], (TOKENS,), VOCAB, 2), jax.random.fold_in(seeds[3], 3), 0, VOCAB - 1).astype(jnp.int32)
    segments = jnp.searchsorted(jnp.cumsum(ragged_sizes(seeds[4], SEQS, TOKENS, TOKENS // 2, 2)), jnp.arange(TOKENS), side="right").astype(jnp.int32)
    scored = draw_scored(jax.random.fold_in(seeds[6], 71), 0)
    return {"hidden": hidden, "norm_gain": norm_gain, "lm_head": lm_head, "targets": targets, "segments": segments, "scored": scored}


def reference(hidden, norm_gain, lm_head, targets, segments, scored):
    values = hidden.astype(jnp.float32)
    row_scale = lax.rsqrt(lax.optimization_barrier(jnp.mean(values * values, axis=1, keepdims=True)) + 1e-05)
    normed = (values * row_scale * norm_gain.astype(jnp.float32)[None, :]).astype(jnp.bfloat16)
    col_width = lm_head.shape[1]
    block_width = math.gcd(col_width, 8192)
    block_count = col_width // block_width
    row_count = hidden.shape[0]

    def advance(running, block_index):
        row_top, row_total, row_weighted, picked = running
        first_col = (block_index * block_width).astype(jnp.int32)
        weights = lax.dynamic_slice_in_dim(lm_head, first_col, block_width, 1)
        logits = jnp.dot(normed, weights, preferred_element_type=jnp.float32)
        new_top = jnp.maximum(row_top, lax.optimization_barrier(jnp.max(logits, axis=1)))
        old_scale = jnp.exp(row_top - new_top)
        scaled = jnp.exp(logits - new_top[:, None])
        row_total = row_total * old_scale + lax.optimization_barrier(jnp.sum(scaled, axis=1))
        row_weighted = row_weighted * old_scale + lax.optimization_barrier(jnp.sum(scaled * logits, axis=1))
        columns = first_col + jnp.arange(block_width, dtype=jnp.int32)
        picked = picked + lax.optimization_barrier(jnp.sum(jnp.where(columns[None, :] == targets[:, None], logits, jnp.float32(0.0)), axis=1))
        return ((new_top, row_total, row_weighted, picked), None)
    start_state = (jnp.full((row_count,), -jnp.inf, jnp.float32), jnp.zeros((row_count,), jnp.float32), jnp.zeros((row_count,), jnp.float32), jnp.zeros((row_count,), jnp.float32))
    final_state, unused = lax.scan(advance, start_state, jnp.arange(block_count, dtype=jnp.int32))
    row_top, row_total, row_weighted, picked = final_state
    log_norm = row_top + jnp.log(row_total)
    row_flags = scored.astype(jnp.float32)
    token_logprob = row_flags * (picked - log_norm)
    token_entropy = row_flags * (log_norm - row_weighted / row_total)
    seq_ids = jnp.arange(SEQS, dtype=jnp.int32)
    seq_logprob = lax.optimization_barrier(jnp.sum(jnp.where(segments[None, :] == seq_ids[:, None], token_logprob[None, :], jnp.float32(0.0)), axis=1))
    return (token_logprob, token_entropy, seq_logprob)
```

```python
import jax
import jax.numpy as jnp
from jax import lax
from jax.sharding import PartitionSpec as P

SEQS = 4
SCORE_MOST = 4


def local(hidden, norm_gain, lm_head, targets, segments, scored):
    col_width = lm_head.shape[1]
    own_index = lax.axis_index("req")
    first_col = (own_index * lax.axis_size("tp") + lax.axis_index("tp")) * col_width
    rank = jnp.cumsum(scored) - 1
    slots = jnp.arange(SCORE_MOST, dtype=jnp.int32)
    chosen = (scored[None, :] == 1) & (rank[None, :] == slots[:, None])
    values = jnp.sum(
        jnp.where(chosen[:, :, None], hidden.astype(jnp.float32)[None, :, :], 0.0), axis=1
    )
    row_scale = lax.rsqrt(jnp.mean(values * values, axis=1, keepdims=True) + 1e-05)
    normed = (values * row_scale * norm_gain.astype(jnp.float32)[None, :]).astype(jnp.bfloat16)
    codes = jnp.sum(jnp.where(chosen, (targets * SEQS + segments + 1)[None, :], 0), axis=1) - 1
    rows, row_codes = lax.all_gather((normed, codes), "req", axis=0, tiled=True)
    used = row_codes >= 0
    row_targets = row_codes // SEQS
    row_segments = row_codes % SEQS
    logits = jnp.dot(rows, lm_head, preferred_element_type=jnp.float32)
    own_top = jnp.max(logits, axis=1)
    scaled = jnp.exp(logits - own_top[:, None])
    own_total = jnp.sum(scaled, axis=1)
    own_weighted = jnp.sum(scaled * logits, axis=1)
    columns = first_col + jnp.arange(col_width, dtype=jnp.int32)
    own_picked = jnp.sum(jnp.where(columns[None, :] == row_targets[:, None], logits, 0.0), axis=1)
    row_top = lax.pmax(own_top, ("req", "tp"))
    factor = jnp.exp(own_top - row_top)
    sums = lax.psum(jnp.stack([own_total * factor, own_weighted * factor, own_picked]), ("req", "tp"))
    log_norm = row_top + jnp.log(sums[0])
    logprob = jnp.where(used, sums[2] - log_norm, 0.0)
    entropy = jnp.where(used, log_norm - sums[1] / sums[0], 0.0)
    seq_ids = jnp.arange(SEQS, dtype=jnp.int32)
    seq_logprob = jnp.sum(
        jnp.where(row_segments[None, :] == seq_ids[:, None], logprob[None, :], 0.0), axis=1
    )
    own = own_index * SCORE_MOST
    own_logprob = lax.dynamic_slice_in_dim(logprob, own, SCORE_MOST, 0)
    own_entropy = lax.dynamic_slice_in_dim(entropy, own, SCORE_MOST, 0)
    token_logprob = jnp.sum(jnp.where(chosen, own_logprob[:, None], 0.0), axis=0)
    token_entropy = jnp.sum(jnp.where(chosen, own_entropy[:, None], 0.0), axis=0)
    return (token_logprob, token_entropy, seq_logprob)


def solution(mesh):
    return jax.shard_map(
        local,
        mesh=mesh,
        in_specs=(P("req", None), P(), P(None, ("req", "tp")), P("req"), P("req"), P("req")),
        out_specs=(P("req"), P("req"), P()),
        check_vma=False,
    )
```

```python
import jax
import jax.numpy as jnp
from jax import lax
from jax.experimental import pallas as pl
from jax.experimental.pallas import tpu as pltpu
from jax.sharding import PartitionSpec as P

SEQS = 4
SLOTS = 4
RING = 8
TP = 4
ROWS = 8
MESH = pl.DeviceIdType.MESH


def ring_distance(offset):
    return min(offset, RING - offset)


def forward_hops(length_up, offset):
    hops = []
    if offset < length_up:
        hops.append((offset + 1, 1))
    down = RING - 1 - length_up
    travelled = (RING - offset) % RING
    if (offset == 0 or offset > length_up) and travelled < down:
        hops.append(((offset - 1) % RING, -1))
    return hops


def joined(stats, lane):
    tops = jnp.max(jnp.where(lane == 0, stats, -jnp.inf), axis=-1, keepdims=True)
    top = jnp.max(tops, axis=0, keepdims=True)
    factor = jnp.where(lane == 3, 1.0, jnp.exp(tops - top))
    sums = jnp.sum(stats * factor, axis=0)
    return jnp.where(lane[0] == 0, top[0], sums)


def kernel(
    targets_ref, segments_ref, scored_ref, hidden_ref, gain_ref, head_ref,
    out_ref,
    rows, heads, stats, inbox_a, joined_a, inbox_b, inbox_x, parts_a, parts_b, sum_b, other_part,
    row_send, row_recv, head_sem, misc_send, misc_recv,
):
    depth, width = head_ref.shape
    req, tp = lax.axis_index("req"), lax.axis_index("tp")
    core = req % 2
    first = (req // 2) % RING
    second = req // (2 * RING)
    pos_a = first + core * (second - first)
    pos_b = second + core * (first - second)
    stride_a = 2 + core * (2 * RING - 2)
    stride_b = 2 * RING - core * (2 * RING - 2)

    def along_a(offset):
        return (req + ((pos_a + offset + RING) % RING - pos_a) * stride_a, tp)

    def along_b(offset):
        return (req + ((pos_b + offset + RING) % RING - pos_b) * stride_b, tp)

    def along_x(offset):
        return (req, (tp + offset) % TP)

    partner = (req + 1 - 2 * core, tp)

    def remote(source, target, send_sem, recv_sem, device):
        return pltpu.make_async_remote_copy(
            src_ref=source, dst_ref=target, send_sem=send_sem, recv_sem=recv_sem,
            device_id=device, device_id_type=MESH,
        )

    barrier = pltpu.get_barrier_semaphore()
    greeted = [along_a(1), along_a(-1), along_b(1), along_b(-1), partner] + [along_x(d) for d in (1, 2, 3)]
    for device in greeted:
        pl.semaphore_signal(barrier, inc=1, device_id=device, device_id_type=MESH)

    own_head = pltpu.make_async_copy(head_ref, heads.at[0], head_sem.at[0])
    own_head.start()

    slot_of, taken = [], 0
    for r in range(ROWS):
        flag = scored_ref[r]
        slot_of.append(flag * (taken + 1) - 1)
        taken = taken + flag
    hidden = hidden_ref[...].astype(jnp.float32)
    slot_row = lax.broadcasted_iota(jnp.int32, (SLOTS, depth), 0)
    values = jnp.zeros((SLOTS, depth), jnp.float32)
    slot_id = lax.broadcasted_iota(jnp.int32, (SLOTS, 128), 0)
    lane_id = lax.broadcasted_iota(jnp.int32, (SLOTS, 128), 1)
    ids = jnp.zeros((SLOTS, 128), jnp.int32)
    for r in range(ROWS):
        values = jnp.where(slot_row == slot_of[r], hidden[r : r + 1, :], values)
        ids = jnp.where(slot_id == slot_of[r], targets_ref[r], ids)
    row_scale = lax.rsqrt(jnp.mean(values * values, axis=1, keepdims=True) + 1e-05)
    normed = (values * row_scale * gain_ref[...].astype(jnp.float32)).astype(jnp.bfloat16)
    digits = jnp.where(
        lane_id == 0, ids & 63, jnp.where(lane_id == 1, (ids >> 6) & 63, jnp.where(lane_id == 2, ids >> 12, 0))
    )
    rows[0, :, :depth] = normed
    rows[0, :, depth:] = digits.astype(jnp.float32).astype(jnp.bfloat16)

    pl.semaphore_wait(barrier, len(greeted))

    def row_copy(source, target, device):
        return remote(rows.at[source], rows.at[target], row_send, row_recv.at[target], device)

    def up_length(i):
        return 4 - i % 2

    events = sorted(
        ((i, j) for i in range(RING) for j in range(RING)),
        key=lambda e: (
            ring_distance(e[0]) + (e[1] if e[1] <= up_length(e[0]) else RING - e[1]),
            e[1] != 0,
            ring_distance(e[1]),
        ),
    )
    head_copy = remote(head_ref, heads.at[1], head_sem.at[1], head_sem.at[2], partner)
    for i, j in events:
        slot = i * RING + j
        if slot:
            row_copy(slot, slot, along_b(1)).wait_recv()
        if j == 0:
            for nxt, step in forward_hops(4, i):
                row_copy(slot, nxt * RING, along_a(step)).start()
        for nxt, step in forward_hops(up_length(i), j):
            row_copy(slot, i * RING + nxt, along_b(step)).start()
        if slot == 0:
            head_copy.start()
    own_head.wait()
    head_copy.wait()

    count = RING * RING * SLOTS
    block = rows[...]
    gathered = block[:, :, :depth].reshape(count, depth)
    digit = block[:, :, depth:].astype(jnp.float32).reshape(count, 128)
    lane = lax.broadcasted_iota(jnp.int32, (count, 128), 1)
    worth = jnp.where(lane == 0, 1.0, jnp.where(lane == 1, 64.0, jnp.where(lane == 2, 4096.0, 0.0)))
    row_target = jnp.sum(digit * worth, axis=1, keepdims=True).astype(jnp.int32)
    logits = [jnp.dot(gathered, heads[h], preferred_element_type=jnp.float32) for h in range(2)]
    top = jnp.maximum(
        jnp.max(logits[0], axis=1, keepdims=True), jnp.max(logits[1], axis=1, keepdims=True)
    )
    total = weighted = picked = 0.0
    for h in range(2):
        holder = req + h * (1 - 2 * core)
        column = lax.broadcasted_iota(jnp.int32, (count, width), 1) + (holder * TP + tp) * width
        scaled = jnp.exp(logits[h] - top)
        total = total + jnp.sum(scaled, axis=1, keepdims=True)
        weighted = weighted + jnp.sum(scaled * logits[h], axis=1, keepdims=True)
        picked = picked + jnp.sum(jnp.where(column == row_target, logits[h], 0.0), axis=1, keepdims=True)
    stat = jnp.where(lane == 0, top, jnp.where(lane == 1, total, jnp.where(lane == 2, weighted, picked)))
    stats[...] = stat.reshape(RING, RING, SLOTS, 128)

    sends = []

    def exchange(pairs, send_sem, recv_sem):
        copies = [
            remote(source, target, send_sem.at[n], recv_sem.at[n], device)
            for n, (source, target, device) in enumerate(pairs)
        ]
        for copy in copies:
            copy.start()
        return copies

    def finish(copies):
        for copy in copies:
            copy.wait_recv()
        sends.extend(copies)

    copies = exchange(
        [(stats.at[i], inbox_a.at[i], along_a(-i)) for i in range(1, RING)], misc_send.at[0], misc_recv.at[0]
    )
    inbox_a[0] = stats[0]
    finish(copies)
    lane4 = lax.broadcasted_iota(jnp.int32, (1, RING, SLOTS, 128), 3)
    joined_a[...] = joined(inbox_a[...], lane4)
    copies = exchange(
        [(joined_a.at[j], inbox_b.at[j], along_b(-j)) for j in range(1, RING)], misc_send.at[1], misc_recv.at[1]
    )
    inbox_b[0] = joined_a[0]
    finish(copies)
    lane3 = lax.broadcasted_iota(jnp.int32, (1, SLOTS, 128), 2)
    inbox_x[tp] = joined(inbox_b[...], lane3)
    copies = exchange(
        [(inbox_x.at[tp], inbox_x.at[tp], along_x(d)) for d in range(1, TP)], misc_send.at[2], misc_recv.at[2]
    )
    finish(copies)
    full = joined(inbox_x[...], lane3)

    def member(n):
        return jnp.sum(jnp.where(lane_id == n, full, 0.0), axis=1, keepdims=True)

    log_norm = member(0) + jnp.log(member(1))
    logprob = member(3) - log_norm
    entropy = log_norm - member(2) / member(1)
    row_slot = jnp.full((SLOTS, 128), -1, jnp.int32)
    row_segment = jnp.full((1, 128), -1, jnp.int32)
    lane1 = lax.broadcasted_iota(jnp.int32, (1, 128), 1)
    for r in range(ROWS):
        row_slot = jnp.where(lane_id == r, slot_of[r], row_slot)
        row_segment = jnp.where(lane1 == r, segments_ref[r], row_segment)
    token_logprob = jnp.sum(jnp.where(row_slot == slot_id, logprob, 0.0), axis=0, keepdims=True)
    token_entropy = jnp.sum(jnp.where(row_slot == slot_id, entropy, 0.0), axis=0, keepdims=True)
    part = jnp.zeros((1, 128), jnp.float32)
    for s in range(SEQS):
        amount = jnp.sum(jnp.where(row_segment == s, token_logprob, 0.0), axis=1, keepdims=True)
        part = jnp.where(lane1 == s, amount, part)

    parts_a[pos_a] = part
    finish(
        exchange(
            [(parts_a.at[pos_a], parts_a.at[pos_a], along_a(i)) for i in range(1, RING)],
            misc_send.at[3], misc_recv.at[3],
        )
    )
    parts_b[pos_b] = jnp.sum(parts_a[...], axis=0)
    finish(
        exchange(
            [(parts_b.at[pos_b], parts_b.at[pos_b], along_b(j)) for j in range(1, RING)],
            misc_send.at[4], misc_recv.at[4],
        )
    )
    sum_b[...] = jnp.sum(parts_b[...], axis=0)
    finish(exchange([(sum_b, other_part, partner)], misc_send.at[5], misc_recv.at[5]))
    seq_logprob = sum_b[...] + other_part[...]
    out_ref[0:1, :] = token_logprob
    out_ref[1:2, :] = token_entropy
    out_ref[2:3, :] = seq_logprob

    for copy in sends:
        copy.wait_send()
    everything = rows.at[pl.ds(0, RING * RING - 1)]
    remote(everything, everything, row_send, row_recv.at[0], partner).wait_send()


def local(hidden, norm_gain, lm_head, targets, segments, scored):
    depth, width = lm_head.shape
    row_width = depth + 128
    smem = pl.BlockSpec(memory_space=pltpu.SMEM)
    vmem = pl.BlockSpec(memory_space=pltpu.VMEM)
    result = pl.pallas_call(
        kernel,
        out_shape=jax.ShapeDtypeStruct((8, 128), jnp.float32),
        in_specs=[smem, smem, smem, vmem, vmem, pl.BlockSpec(memory_space=pl.ANY)],
        out_specs=vmem,
        scratch_shapes=[
            pltpu.VMEM((RING * RING, SLOTS, row_width), jnp.bfloat16),
            pltpu.VMEM((2, depth, width), jnp.bfloat16),
            pltpu.VMEM((RING, RING, SLOTS, 128), jnp.float32),
            pltpu.VMEM((RING, RING, SLOTS, 128), jnp.float32),
            pltpu.VMEM((RING, SLOTS, 128), jnp.float32),
            pltpu.VMEM((RING, SLOTS, 128), jnp.float32),
            pltpu.VMEM((TP, SLOTS, 128), jnp.float32),
            pltpu.VMEM((RING, 1, 128), jnp.float32),
            pltpu.VMEM((RING, 1, 128), jnp.float32),
            pltpu.VMEM((1, 128), jnp.float32),
            pltpu.VMEM((1, 128), jnp.float32),
            pltpu.SemaphoreType.DMA,
            pltpu.SemaphoreType.DMA((RING * RING,)),
            pltpu.SemaphoreType.DMA((3,)),
            pltpu.SemaphoreType.DMA((6, RING)),
            pltpu.SemaphoreType.DMA((6, RING)),
        ],
        compiler_params=pltpu.CompilerParams(
            collective_id=0, has_side_effects=True, vmem_limit_bytes=56 * 1024 * 1024
        ),
    )(targets, segments, scored, hidden, norm_gain.reshape(1, depth), lm_head)
    return (result[0, :ROWS], result[1, :ROWS], result[2, :SEQS])


def solution(mesh):
    return jax.shard_map(
        local,
        mesh=mesh,
        in_specs=(P("req", None), P(), P(None, ("req", "tp")), P("req"), P("req"), P("req")),
        out_specs=(P("req"), P("req"), P()),
        check_vma=False,
    )
```

```python
import jax
import jax.numpy as jnp
from jax import lax
from jax.experimental import pallas as pl
from jax.experimental.pallas import tpu as pltpu
from jax.sharding import PartitionSpec as P

SEQS = 4
SLOTS = 4
RING = 8
TP = 4
ROWS = 8
MESH = pl.DeviceIdType.MESH
ORDER = (0, 1, 7, 2, 6, 3, 5, 4)


def joined(stats, lane):
    tops = jnp.max(jnp.where(lane == 0, stats, -jnp.inf), axis=-1, keepdims=True)
    top = jnp.max(tops, axis=0, keepdims=True)
    factor = jnp.where(lane == 3, 1.0, jnp.exp(tops - top))
    sums = jnp.sum(stats * factor, axis=0)
    return jnp.where(lane[0] == 0, top[0], sums)


def kernel(
    targets_ref, segments_ref, scored_ref, hidden_ref, gain_ref, head_ref,
    out_ref,
    rows, heads, stats, inbox_a, joined_a, inbox_b, parts_a, parts_b,
    row_send, row_recv, head_sem, misc_send, misc_recv,
):
    depth, width = head_ref.shape
    req, tp = lax.axis_index("req"), lax.axis_index("tp")
    core = req % 2
    first = (req // 2) % RING
    second = req // (2 * RING)
    pos_a = first + core * (second - first)
    pos_b = second + core * (first - second)
    stride_a = 2 + core * (2 * RING - 2)
    stride_b = 2 * RING - core * (2 * RING - 2)

    def along_a(offset):
        return (req + ((pos_a + offset + RING) % RING - pos_a) * stride_a, tp)

    def along_b(offset):
        return (req + ((pos_b + offset + RING) % RING - pos_b) * stride_b, tp)

    def along_x(offset):
        return (req, (tp + offset) % TP)

    def shifted(device, offset):
        return (device[0], (tp + offset) % TP)

    def across(device):
        return (device[0] + 1 - 2 * core, device[1])

    partner = across((req, tp))

    def remote(source, target, send_sem, recv_sem, device):
        return pltpu.make_async_remote_copy(
            src_ref=source, dst_ref=target, send_sem=send_sem, recv_sem=recv_sem,
            device_id=device, device_id_type=MESH,
        )

    barrier = pltpu.get_barrier_semaphore()
    greeted = [along_a(ORDER[p]) for p in range(RING - 1, 0, -1)] + [along_b(j) for j in (2, -2, 1, -1)]
    greeted += [along_x(d) for d in (2, 1, 3)] + [partner]
    for device in greeted:
        pl.semaphore_signal(barrier, inc=1, device_id=device, device_id_type=MESH)

    own_head = pltpu.make_async_copy(head_ref, heads.at[0], head_sem.at[0])
    own_head.start()

    slot_of, taken = [], 0
    for r in range(ROWS):
        flag = scored_ref[r]
        slot_of.append(flag * (taken + 1) - 1)
        taken = taken + flag
    hidden = hidden_ref[...].astype(jnp.float32)
    slot_row = lax.broadcasted_iota(jnp.int32, (SLOTS, depth), 0)
    values = jnp.zeros((SLOTS, depth), jnp.float32)
    slot_id = lax.broadcasted_iota(jnp.int32, (SLOTS, 128), 0)
    lane_id = lax.broadcasted_iota(jnp.int32, (SLOTS, 128), 1)
    ids = jnp.zeros((SLOTS, 128), jnp.int32)
    for r in range(ROWS):
        values = jnp.where(slot_row == slot_of[r], hidden[r : r + 1, :], values)
        ids = jnp.where(slot_id == slot_of[r], targets_ref[r], ids)
    row_scale = lax.rsqrt(jnp.mean(values * values, axis=1, keepdims=True) + 1e-05)
    gain = gain_ref[...].astype(jnp.float32)
    gain = jnp.concatenate([gain[k : k + 1, :] for k in range(depth // 128)], axis=1)
    normed = (values * row_scale * gain).astype(jnp.bfloat16)
    digits = jnp.where(
        lane_id == 0, ids & 63, jnp.where(lane_id == 1, (ids >> 6) & 63, jnp.where(lane_id == 2, ids >> 12, 0))
    )
    rows[0, :, :depth] = normed
    rows[0, :, depth:] = digits.astype(jnp.float32).astype(jnp.bfloat16)

    pl.semaphore_wait(barrier, len(greeted))

    def row_copy(source, target, device):
        return remote(rows.at[source], rows.at[target], row_send, row_recv.at[target], device)

    def arrived(slot):
        row_copy(slot, slot, along_b(1)).wait_recv()

    for p in range(1, RING):
        row_copy(0, p, along_a(ORDER[p])).start()
    head_copy = remote(head_ref, heads.at[1], head_sem.at[1], head_sem.at[2], partner)
    for p in range(RING):
        if p:
            arrived(p)
        for step in (2, -2, 1, -1):
            row_copy(p, (step % RING) * RING + p, along_b(step)).start()
        if p == 0:
            head_copy.start()
    for p in range(RING):
        for side in (1, -1):
            slot = (2 * side) % RING * RING + p
            arrived(slot)
            if side == (1 if p % 2 else -1):
                row_copy(slot, 4 * RING + p, along_b(2 * side)).start()
            row_copy(slot, (3 * side) % RING * RING + p, along_b(side)).start()
    for j in (1, 7, 3, 5, 4):
        for p in range(RING):
            arrived(j * RING + p)
    own_head.wait()
    head_copy.wait()

    count = RING * RING * SLOTS
    block = rows[...]
    gathered = block[:, :, :depth].reshape(count, depth)
    digit = block[:, :, depth:].astype(jnp.float32).reshape(count, 128)
    lane = lax.broadcasted_iota(jnp.int32, (count, 128), 1)
    worth = jnp.where(lane == 0, 1.0, jnp.where(lane == 1, 64.0, jnp.where(lane == 2, 4096.0, 0.0)))
    row_target = jnp.sum(digit * worth, axis=1, keepdims=True).astype(jnp.int32)
    logits = [jnp.dot(gathered, heads[h], preferred_element_type=jnp.float32) for h in range(2)]
    top = jnp.maximum(
        jnp.max(logits[0], axis=1, keepdims=True), jnp.max(logits[1], axis=1, keepdims=True)
    )
    total = weighted = picked = 0.0
    for h in range(2):
        holder = req + h * (1 - 2 * core)
        column = lax.broadcasted_iota(jnp.int32, (count, width), 1) + (holder * TP + tp) * width
        scaled = jnp.exp(logits[h] - top)
        total = total + jnp.sum(scaled, axis=1, keepdims=True)
        weighted = weighted + jnp.sum(scaled * logits[h], axis=1, keepdims=True)
        picked = picked + jnp.sum(jnp.where(column == row_target, logits[h], 0.0), axis=1, keepdims=True)
    stat = jnp.where(lane == 0, top, jnp.where(lane == 1, total, jnp.where(lane == 2, weighted, picked)))
    stats[...] = stat.reshape(RING, RING, SLOTS, 128)

    sends = []

    def exchange(pairs, phase):
        copies = [
            remote(source, target, misc_send.at[phase, n], misc_recv.at[phase, n], device)
            for n, (source, target, device) in enumerate(pairs)
        ]
        for copy in copies:
            copy.start()
        return copies

    def finish(copies):
        for copy in copies:
            copy.wait_recv()
        sends.extend(copies)

    copies = exchange(
        [(stats.at[:, p], inbox_a.at[p], along_a(-ORDER[p])) for p in range(RING - 1, 0, -1)], 0
    )
    inbox_a[0] = stats[:, 0]
    finish(copies)
    lane4 = lax.broadcasted_iota(jnp.int32, (1, RING, SLOTS, 128), 3)
    joined_a[...] = joined(inbox_a[...], lane4)
    copies = exchange(
        [
            (joined_a.at[j], inbox_b.at[tp, j], shifted(along_b(-j), d))
            for j in (4, 3, 5, 2, 6, 1, 7, 0)
            for d in (2, 1, 3, 0)
            if j or d
        ],
        1,
    )
    inbox_b[tp, 0] = joined_a[0]
    finish(copies)
    lane3 = lax.broadcasted_iota(jnp.int32, (1, SLOTS, 128), 2)
    full = joined(inbox_b[...].reshape(TP * RING, SLOTS, 128), lane3)

    def member(n):
        return jnp.sum(jnp.where(lane_id == n, full, 0.0), axis=1, keepdims=True)

    log_norm = member(0) + jnp.log(member(1))
    logprob = member(3) - log_norm
    entropy = log_norm - member(2) / member(1)
    row_slot = jnp.full((SLOTS, 128), -1, jnp.int32)
    row_segment = jnp.full((1, 128), -1, jnp.int32)
    lane1 = lax.broadcasted_iota(jnp.int32, (1, 128), 1)
    for r in range(ROWS):
        row_slot = jnp.where(lane_id == r, slot_of[r], row_slot)
        row_segment = jnp.where(lane1 == r, segments_ref[r], row_segment)
    token_logprob = jnp.sum(jnp.where(row_slot == slot_id, logprob, 0.0), axis=0, keepdims=True)
    token_entropy = jnp.sum(jnp.where(row_slot == slot_id, entropy, 0.0), axis=0, keepdims=True)
    part = jnp.zeros((1, 128), jnp.float32)
    for s in range(SEQS):
        amount = jnp.sum(jnp.where(row_segment == s, token_logprob, 0.0), axis=1, keepdims=True)
        part = jnp.where(lane1 == s, amount, part)

    parts_a[pos_a] = part
    finish(exchange([(parts_a.at[pos_a], parts_a.at[pos_a], along_a(ORDER[p])) for p in range(RING - 1, 0, -1)], 2))
    parts_b[core, pos_b] = jnp.sum(parts_a[...], axis=0)
    mine = parts_b.at[core, pos_b]
    finish(
        exchange(
            [
                (mine, mine, other)
                for p in range(RING - 1, -1, -1)
                for other in (along_b(ORDER[p]), across(along_b(ORDER[p])))
            ][:-2]
            + [(mine, mine, partner)],
            3,
        )
    )
    seq_logprob = jnp.sum(parts_b[...].reshape(2 * RING, 1, 128), axis=0)
    out_ref[0:1, :] = token_logprob
    out_ref[1:2, :] = token_entropy
    out_ref[2:3, :] = seq_logprob

    for copy in sends:
        copy.wait_send()
    everything = rows.at[pl.ds(0, RING * RING - 1)]
    remote(everything, everything, row_send, row_recv.at[0], partner).wait_send()


def split_kernel(result_ref, logprob_ref, entropy_ref, seq_ref):
    logprob_ref[...] = result_ref[0, :ROWS]
    entropy_ref[...] = result_ref[1, :ROWS]
    seq_ref[...] = result_ref[2, :SEQS]


def local(hidden, norm_gain, lm_head, targets, segments, scored):
    depth, width = lm_head.shape
    row_width = depth + 128
    smem = pl.BlockSpec(memory_space=pltpu.SMEM)
    vmem = pl.BlockSpec(memory_space=pltpu.VMEM)
    result = pl.pallas_call(
        kernel,
        out_shape=jax.ShapeDtypeStruct((8, 128), jnp.float32),
        in_specs=[smem, smem, smem, vmem, vmem, pl.BlockSpec(memory_space=pl.ANY)],
        out_specs=vmem,
        scratch_shapes=[
            pltpu.VMEM((RING * RING, SLOTS, row_width), jnp.bfloat16),
            pltpu.VMEM((2, depth, width), jnp.bfloat16),
            pltpu.VMEM((RING, RING, SLOTS, 128), jnp.float32),
            pltpu.VMEM((RING, RING, SLOTS, 128), jnp.float32),
            pltpu.VMEM((RING, SLOTS, 128), jnp.float32),
            pltpu.VMEM((TP, RING, SLOTS, 128), jnp.float32),
            pltpu.VMEM((RING, 1, 128), jnp.float32),
            pltpu.VMEM((2, RING, 1, 128), jnp.float32),
            pltpu.SemaphoreType.DMA,
            pltpu.SemaphoreType.DMA((RING * RING,)),
            pltpu.SemaphoreType.DMA((3,)),
            pltpu.SemaphoreType.DMA((4, TP * RING)),
            pltpu.SemaphoreType.DMA((4, TP * RING)),
        ],
        compiler_params=pltpu.CompilerParams(
            collective_id=0, has_side_effects=True, vmem_limit_bytes=56 * 1024 * 1024
        ),
    )(targets, segments, scored, hidden, norm_gain.reshape(depth // 128, 128), lm_head)
    return pl.pallas_call(
        split_kernel,
        out_shape=[jax.ShapeDtypeStruct((n,), jnp.float32) for n in (ROWS, ROWS, SEQS)],
        in_specs=[vmem],
        out_specs=[vmem, vmem, vmem],
    )(result)


def solution(mesh):
    return jax.shard_map(
        local,
        mesh=mesh,
        in_specs=(P("req", None), P(), P(None, ("req", "tp")), P("req"), P("req"), P("req")),
        out_specs=(P("req"), P("req"), P()),
        check_vma=False,
    )
```

```python
import jax
import jax.numpy as jnp
from jax import lax
from jax.experimental import pallas as pl
from jax.experimental.pallas import tpu as pltpu
from jax.sharding import PartitionSpec as P

SEQS = 4
SLOTS = 4
RING = 8
TP = 4
ROWS = 8
GROUP = SLOTS * RING
MESH = pl.DeviceIdType.MESH
ORDER = (0, 1, 7, 2, 6, 3, 5, 4)


def joined(stats):
    tops, sums = stats[..., 0:1, :], stats[..., 1:2, :]
    top = jnp.max(tops, axis=0)
    lane = lax.broadcasted_iota(jnp.int32, tops.shape, tops.ndim - 1)
    factor = jnp.where(lane >= 2 * GROUP, 1.0, jnp.exp(tops - top))
    return top, jnp.sum(sums * factor, axis=0)


def kernel(
    targets_ref, segments_ref, scored_ref, hidden_ref, gain_ref, head_ref,
    out_ref,
    rows, heads, stats, inbox_a, inbox_b, parts,
    row_send, row_recv, head_sem, misc_send, misc_recv,
):
    depth, width = head_ref.shape
    req, tp = lax.axis_index("req"), lax.axis_index("tp")
    core = req % 2
    first = (req // 2) % RING
    second = req // (2 * RING)
    pos_a = first + core * (second - first)
    pos_b = second + core * (first - second)
    stride_a = 2 + core * (2 * RING - 2)
    stride_b = 2 * RING - core * (2 * RING - 2)

    def along_a(offset):
        return (req + ((pos_a + offset + RING) % RING - pos_a) * stride_a, tp)

    def along_b(offset):
        return (req + ((pos_b + offset + RING) % RING - pos_b) * stride_b, tp)

    def along_x(offset):
        return (req, (tp + offset) % TP)

    def shifted(device, offset):
        return (device[0], (tp + offset) % TP)

    def across(device):
        return (device[0] + 1 - 2 * core, device[1])

    partner = across((req, tp))

    def remote(source, target, send_sem, recv_sem, device):
        return pltpu.make_async_remote_copy(
            src_ref=source, dst_ref=target, send_sem=send_sem, recv_sem=recv_sem,
            device_id=device, device_id_type=MESH,
        )

    barrier = pltpu.get_barrier_semaphore()
    greeted = [along_a(ORDER[p]) for p in range(RING - 1, 0, -1)] + [along_b(j) for j in (2, -2, 1, -1)]
    greeted += [along_x(d) for d in (2, 1, 3)] + [partner]
    for device in greeted:
        pl.semaphore_signal(barrier, inc=1, device_id=device, device_id_type=MESH)

    own_head = pltpu.make_async_copy(head_ref, heads.at[0], head_sem.at[0])
    own_head.start()

    slot_of, taken = [], 0
    for r in range(ROWS):
        flag = scored_ref[r]
        slot_of.append(flag * (taken + 1) - 1)
        taken = taken + flag
    hidden = hidden_ref[...].astype(jnp.float32)
    slot_row = lax.broadcasted_iota(jnp.int32, (SLOTS, depth), 0)
    values = jnp.zeros((SLOTS, depth), jnp.float32)
    slot_id = lax.broadcasted_iota(jnp.int32, (SLOTS, 128), 0)
    lane_id = lax.broadcasted_iota(jnp.int32, (SLOTS, 128), 1)
    ids = jnp.zeros((SLOTS, 128), jnp.int32)
    codes = jnp.zeros((SLOTS, 128), jnp.int32)
    for r in range(ROWS):
        values = jnp.where(slot_row == slot_of[r], hidden[r : r + 1, :], values)
        ids = jnp.where(slot_id == slot_of[r], targets_ref[r], ids)
        codes = jnp.where(slot_id == slot_of[r], segments_ref[r] + 1, codes)
    row_scale = lax.rsqrt(jnp.mean(values * values, axis=1, keepdims=True) + 1e-05)
    gain = gain_ref[...].astype(jnp.float32)
    gain = jnp.concatenate([gain[k : k + 1, :] for k in range(depth // 128)], axis=1)
    normed = (values * row_scale * gain).astype(jnp.bfloat16)
    digits = jnp.where(
        lane_id == 0, ids & 63, jnp.where(lane_id == 1, (ids >> 6) & 63, jnp.where(lane_id == 2, ids >> 12, 0))
    )
    rows[0, :, :depth] = normed
    rows[0, :, depth:] = digits.astype(jnp.float32).astype(jnp.bfloat16)

    pl.semaphore_wait(barrier, len(greeted))

    def row_copy(source, target, device):
        return remote(rows.at[source], rows.at[target], row_send, row_recv.at[target], device)

    def arrived(slot):
        row_copy(slot, slot, along_b(1)).wait_recv()

    for p in range(1, RING):
        row_copy(0, p, along_a(ORDER[p])).start()
    head_copy = remote(head_ref, heads.at[1], head_sem.at[1], head_sem.at[2], partner)
    for p in range(RING):
        if p:
            arrived(p)
        for step in (2, -2, 1, -1):
            row_copy(p, (step % RING) * RING + p, along_b(step)).start()
        if p == 0:
            head_copy.start()
    for p in range(RING):
        for side in (1, -1):
            slot = (2 * side) % RING * RING + p
            arrived(slot)
            if side == (1 if p % 2 else -1):
                row_copy(slot, 4 * RING + p, along_b(2 * side)).start()
            row_copy(slot, (3 * side) % RING * RING + p, along_b(side)).start()
    for j in (1, 7, 3, 5, 4):
        for p in range(RING):
            arrived(j * RING + p)
    own_head.wait()
    head_copy.wait()

    count = RING * RING * SLOTS
    block = rows[...]
    gathered = block[:, :, :depth].reshape(count, depth)
    digit = block[:, :, depth:].astype(jnp.float32).reshape(count, 128)
    lane = lax.broadcasted_iota(jnp.int32, (count, 128), 1)
    worth = jnp.where(lane == 0, 1.0, jnp.where(lane == 1, 64.0, jnp.where(lane == 2, 4096.0, 0.0)))
    row_target = jnp.sum(digit * worth, axis=1, keepdims=True).astype(jnp.int32)
    logits = [jnp.dot(gathered, heads[h], preferred_element_type=jnp.float32) for h in range(2)]
    top = jnp.maximum(
        jnp.max(logits[0], axis=1, keepdims=True), jnp.max(logits[1], axis=1, keepdims=True)
    )
    total = weighted = picked = 0.0
    for h in range(2):
        holder = req + h * (1 - 2 * core)
        column = lax.broadcasted_iota(jnp.int32, (count, width), 1) + (holder * TP + tp) * width
        scaled = jnp.exp(logits[h] - top)
        total = total + jnp.sum(scaled, axis=1, keepdims=True)
        weighted = weighted + jnp.sum(scaled * logits[h], axis=1, keepdims=True)
        picked = picked + jnp.sum(jnp.where(column == row_target, logits[h], 0.0), axis=1, keepdims=True)
    row = lax.broadcasted_iota(jnp.int32, (count, 128), 0)
    owner_b = (pos_b + RING - row // GROUP) % RING
    own_lane = lane % GROUP == owner_b * SLOTS + row % SLOTS
    sums = jnp.where(lane < GROUP, total, jnp.where(lane < 2 * GROUP, weighted, picked))

    def in_lanes(value, end):
        kept = jnp.where(own_lane & (lane < end), value, 0.0).reshape(RING, RING, SLOTS, 128)
        return jnp.sum(jnp.sum(kept, axis=0), axis=1, keepdims=True)

    code_lane = (lane_id == 3 * GROUP + pos_b * SLOTS + slot_id) & (tp == 0)
    code = jnp.sum(jnp.where(code_lane, codes, 0).astype(jnp.float32), axis=0, keepdims=True)
    stats[:, 0:1, :] = in_lanes(top, 2 * GROUP)
    stats[:, 1:2, :] = in_lanes(sums, 3 * GROUP)
    stats[0, 1:2, :] = stats[0, 1:2, :] + code

    sends = []

    def exchange(pairs, phase):
        copies = [
            remote(source, target, misc_send.at[phase, n], misc_recv.at[phase, n], device)
            for n, (source, target, device) in enumerate(pairs)
        ]
        for copy in copies:
            copy.start()
        return copies

    def finish(copies):
        for copy in copies:
            copy.wait_recv()
        sends.extend(copies)

    copies = exchange(
        [(stats.at[p], inbox_a.at[p], along_a(-ORDER[p])) for p in range(RING - 1, 0, -1)], 0
    )
    inbox_a[0] = stats[0]
    finish(copies)
    inbox_b[tp, pos_b, 0:1, :], inbox_b[tp, pos_b, 1:2, :] = joined(inbox_a[...])
    mine = inbox_b.at[tp, pos_b]
    finish(
        exchange(
            [
                (mine, mine, shifted(along_b(j), d))
                for j in (4, 3, 5, 2, 6, 1, 7, 0)
                for d in (2, 1, 3, 0)
                if j or d
            ],
            1,
        )
    )
    full_top, full_sums = joined(inbox_b[...].reshape(TP * RING, 2, 128))
    row_id = lax.broadcasted_iota(jnp.int32, (GROUP, 128), 0)
    row_lane = lax.broadcasted_iota(jnp.int32, (GROUP, 128), 1)

    def member(value, n):
        return jnp.sum(jnp.where(row_lane == row_id + n * GROUP, value, 0.0), axis=1, keepdims=True)

    full_total = member(full_sums, 0)
    log_norm = member(full_top, 0) + jnp.log(full_total)
    logprob = member(full_sums, 2) - log_norm
    entropy = log_norm - member(full_sums, 1) / full_total
    row_code = member(full_sums, 3).astype(jnp.int32)
    part = jnp.sum(jnp.where(row_code == row_lane + 1, logprob, 0.0), axis=0, keepdims=True)

    parts[core, pos_a] = part
    own_sum = parts.at[core, pos_a]
    copies = exchange(
        [
            (own_sum, own_sum, other)
            for p in range(RING - 1, 0, -1)
            for other in (along_a(ORDER[p]), across(along_a(ORDER[p])))
        ]
        + [(own_sum, own_sum, partner)],
        2,
    )
    row_slot = jnp.full((GROUP, 128), -1, jnp.int32)
    for r in range(ROWS):
        row_slot = jnp.where(row_lane == r, slot_of[r], row_slot)
    own_row = (row_slot >= 0) & (row_id == row_slot + pos_b * SLOTS)
    token_logprob = jnp.sum(jnp.where(own_row, logprob, 0.0), axis=0, keepdims=True)
    token_entropy = jnp.sum(jnp.where(own_row, entropy, 0.0), axis=0, keepdims=True)
    finish(copies)
    seq_logprob = jnp.sum(parts[...].reshape(2 * RING, 1, 128), axis=0)
    out_ref[0:1, :] = token_logprob
    out_ref[1:2, :] = token_entropy
    out_ref[2:3, :] = seq_logprob

    for copy in sends:
        copy.wait_send()
    everything = rows.at[pl.ds(0, RING * RING - 1)]
    remote(everything, everything, row_send, row_recv.at[0], partner).wait_send()


def split_kernel(result_ref, logprob_ref, entropy_ref, seq_ref):
    logprob_ref[...] = result_ref[0, :ROWS]
    entropy_ref[...] = result_ref[1, :ROWS]
    seq_ref[...] = result_ref[2, :SEQS]


def local(hidden, norm_gain, lm_head, targets, segments, scored):
    depth, width = lm_head.shape
    row_width = depth + 128
    smem = pl.BlockSpec(memory_space=pltpu.SMEM)
    vmem = pl.BlockSpec(memory_space=pltpu.VMEM)
    result = pl.pallas_call(
        kernel,
        out_shape=jax.ShapeDtypeStruct((8, 128), jnp.float32),
        in_specs=[smem, smem, smem, vmem, vmem, pl.BlockSpec(memory_space=pl.ANY)],
        out_specs=vmem,
        scratch_shapes=[
            pltpu.VMEM((RING * RING, SLOTS, row_width), jnp.bfloat16),
            pltpu.VMEM((2, depth, width), jnp.bfloat16),
            pltpu.VMEM((RING, 2, 128), jnp.float32),
            pltpu.VMEM((RING, 2, 128), jnp.float32),
            pltpu.VMEM((TP, RING, 2, 128), jnp.float32),
            pltpu.VMEM((2, RING, 1, 128), jnp.float32),
            pltpu.SemaphoreType.DMA,
            pltpu.SemaphoreType.DMA((RING * RING,)),
            pltpu.SemaphoreType.DMA((3,)),
            pltpu.SemaphoreType.DMA((3, TP * RING)),
            pltpu.SemaphoreType.DMA((3, TP * RING)),
        ],
        compiler_params=pltpu.CompilerParams(
            collective_id=0, has_side_effects=True, vmem_limit_bytes=56 * 1024 * 1024
        ),
    )(targets, segments, scored, hidden, norm_gain.reshape(depth // 128, 128), lm_head)
    return pl.pallas_call(
        split_kernel,
        out_shape=[jax.ShapeDtypeStruct((n,), jnp.float32) for n in (ROWS, ROWS, SEQS)],
        in_specs=[vmem],
        out_specs=[vmem, vmem, vmem],
    )(result)


def solution(mesh):
    return jax.shard_map(
        local,
        mesh=mesh,
        in_specs=(P("req", None), P(), P(None, ("req", "tp")), P("req"), P("req"), P("req")),
        out_specs=(P("req"), P("req"), P()),
        check_vma=False,
    )
```

```python
import jax
import jax.numpy as jnp
from jax import lax
from jax.experimental import pallas as pl
from jax.experimental.pallas import tpu as pltpu
from jax.sharding import PartitionSpec as P

SEQS = 4
SLOTS = 4
RING = 8
TP = 4
ROWS = 8
GROUP = SLOTS * RING
MESH = pl.DeviceIdType.MESH
ORDER = (0, 1, 7, 2, 6, 3, 5, 4)


def joined(stats):
    tops, sums = stats[..., 0:1, :], stats[..., 1:2, :]
    top = jnp.max(tops, axis=0)
    lane = lax.broadcasted_iota(jnp.int32, tops.shape, tops.ndim - 1)
    factor = jnp.where(lane >= 2 * GROUP, 1.0, jnp.exp(tops - top))
    return top, jnp.sum(sums * factor, axis=0)


def kernel(
    targets_ref, segments_ref, scored_ref, hidden_ref, gain_ref, head_ref,
    out_ref,
    rows, heads, stats, inbox_a, inbox_b, parts,
    row_send, row_recv, head_sem, misc_send, misc_recv,
):
    depth, width = head_ref.shape
    req, tp = lax.axis_index("req"), lax.axis_index("tp")
    core = req % 2
    first = (req // 2) % RING
    second = req // (2 * RING)
    pos_a = first + core * (second - first)
    pos_b = second + core * (first - second)
    stride_a = 2 + core * (2 * RING - 2)
    stride_b = 2 * RING - core * (2 * RING - 2)

    def along_a(offset):
        return (req + ((pos_a + offset + RING) % RING - pos_a) * stride_a, tp)

    def along_b(offset):
        return (req + ((pos_b + offset + RING) % RING - pos_b) * stride_b, tp)

    def along_x(offset):
        return (req, (tp + offset) % TP)

    def shifted(device, offset):
        return (device[0], (tp + offset) % TP)

    def across(device):
        return (device[0] + 1 - 2 * core, device[1])

    partner = across((req, tp))

    def remote(source, target, send_sem, recv_sem, device):
        return pltpu.make_async_remote_copy(
            src_ref=source, dst_ref=target, send_sem=send_sem, recv_sem=recv_sem,
            device_id=device, device_id_type=MESH,
        )

    barrier = pltpu.get_barrier_semaphore()
    greeted = [along_a(ORDER[p]) for p in range(RING - 1, 0, -1)] + [along_b(j) for j in (2, -2, 1, -1)]
    greeted += [along_x(d) for d in (2, 1, 3)] + [partner]
    for device in greeted:
        pl.semaphore_signal(barrier, inc=1, device_id=device, device_id_type=MESH)

    own_head = pltpu.make_async_copy(head_ref, heads.at[0], head_sem.at[0])
    own_head.start()

    slot_of, taken = [], 0
    for r in range(ROWS):
        flag = scored_ref[r]
        slot_of.append(flag * (taken + 1) - 1)
        taken = taken + flag
    hidden = hidden_ref[...].astype(jnp.float32)
    slot_row = lax.broadcasted_iota(jnp.int32, (SLOTS, depth), 0)
    values = jnp.zeros((SLOTS, depth), jnp.float32)
    slot_id = lax.broadcasted_iota(jnp.int32, (SLOTS, 128), 0)
    lane_id = lax.broadcasted_iota(jnp.int32, (SLOTS, 128), 1)
    ids = jnp.zeros((SLOTS, 128), jnp.int32)
    codes = jnp.zeros((SLOTS, 128), jnp.int32)
    for r in range(ROWS):
        values = jnp.where(slot_row == slot_of[r], hidden[r : r + 1, :], values)
        ids = jnp.where(slot_id == slot_of[r], targets_ref[r], ids)
        codes = jnp.where(slot_id == slot_of[r], segments_ref[r] + 1, codes)
    row_scale = lax.rsqrt(jnp.mean(values * values, axis=1, keepdims=True) + 1e-05)
    gain = gain_ref[...].astype(jnp.float32)
    gain = jnp.concatenate([gain[k : k + 1, :] for k in range(depth // 128)], axis=1)
    normed = (values * row_scale * gain).astype(jnp.bfloat16)
    digits = jnp.where(
        lane_id == 0, ids & 63, jnp.where(lane_id == 1, (ids >> 6) & 63, jnp.where(lane_id == 2, ids >> 12, 0))
    )
    rows[0, :, :depth] = normed
    rows[0, :, depth:] = digits.astype(jnp.float32).astype(jnp.bfloat16)

    pl.semaphore_wait(barrier, len(greeted))

    def row_copy(source, target, device):
        return remote(rows.at[source], rows.at[target], row_send, row_recv.at[target], device)

    def arrived(slot):
        row_copy(slot, slot, along_b(1)).wait_recv()

    def spread(p):
        for step in (1, -1, 2, -2):
            row_copy(p, (step % RING) * RING + p, along_b(step)).start()

    for p in range(1, RING):
        if p == 3:
            spread(0)
        row_copy(0, p, along_a(ORDER[p])).start()
    head_copy = remote(head_ref, heads.at[1], head_sem.at[1], head_sem.at[2], partner)
    for p in range(RING):
        if p:
            arrived(p)
            spread(p)
        if p == 0:
            head_copy.start()
    for p in range(RING):
        for side in (1, -1):
            slot = (2 * side) % RING * RING + p
            arrived(slot)
            if side == (1 if p % 2 else -1):
                row_copy(slot, 4 * RING + p, along_b(2 * side)).start()
            row_copy(slot, (3 * side) % RING * RING + p, along_b(side)).start()
    for j in (1, 7, 3, 5, 4):
        for p in range(RING):
            arrived(j * RING + p)
    own_head.wait()
    head_copy.wait()

    count = RING * RING * SLOTS
    block = rows[...]
    gathered = block[:, :, :depth].reshape(count, depth)
    digit = block[:, :, depth:].astype(jnp.float32).reshape(count, 128)
    lane = lax.broadcasted_iota(jnp.int32, (count, 128), 1)
    worth = jnp.where(lane == 0, 1.0, jnp.where(lane == 1, 64.0, jnp.where(lane == 2, 4096.0, 0.0)))
    row_target = jnp.sum(digit * worth, axis=1, keepdims=True).astype(jnp.int32)
    logits = [jnp.dot(gathered, heads[h], preferred_element_type=jnp.float32) for h in range(2)]
    top = jnp.maximum(
        jnp.max(logits[0], axis=1, keepdims=True), jnp.max(logits[1], axis=1, keepdims=True)
    )
    total = weighted = picked = 0.0
    for h in range(2):
        holder = req + h * (1 - 2 * core)
        column = lax.broadcasted_iota(jnp.int32, (count, width), 1) + (holder * TP + tp) * width
        scaled = jnp.exp(logits[h] - top)
        total = total + jnp.sum(scaled, axis=1, keepdims=True)
        weighted = weighted + jnp.sum(scaled * logits[h], axis=1, keepdims=True)
        picked = picked + jnp.sum(jnp.where(column == row_target, logits[h], 0.0), axis=1, keepdims=True)
    row = lax.broadcasted_iota(jnp.int32, (count, 128), 0)
    owner_b = (pos_b + RING - row // GROUP) % RING
    own_lane = lane % GROUP == owner_b * SLOTS + row % SLOTS
    sums = jnp.where(lane < GROUP, total, jnp.where(lane < 2 * GROUP, weighted, picked))

    def in_lanes(value, end):
        kept = jnp.where(own_lane & (lane < end), value, 0.0).reshape(RING, RING, SLOTS, 128)
        return jnp.sum(jnp.sum(kept, axis=0), axis=1, keepdims=True)

    code_lane = (lane_id == 3 * GROUP + pos_b * SLOTS + slot_id) & (tp == 0)
    code = jnp.sum(jnp.where(code_lane, codes, 0).astype(jnp.float32), axis=0, keepdims=True)
    stats[:, 0:1, :] = in_lanes(top, 2 * GROUP)
    stats[:, 1:2, :] = in_lanes(sums, 3 * GROUP)
    stats[0, 1:2, :] = stats[0, 1:2, :] + code

    sends = []

    def exchange(pairs, phase):
        copies = [
            remote(source, target, misc_send.at[phase, n], misc_recv.at[phase, n], device)
            for n, (source, target, device) in enumerate(pairs)
        ]
        for copy in copies:
            copy.start()
        return copies

    def finish(copies):
        for copy in copies:
            copy.wait_recv()
        sends.extend(copies)

    copies = exchange(
        [(stats.at[p], inbox_a.at[p], along_a(-ORDER[p])) for p in range(RING - 1, 0, -1)], 0
    )
    inbox_a[0] = stats[0]
    finish(copies)
    inbox_b[tp, pos_b, 0:1, :], inbox_b[tp, pos_b, 1:2, :] = joined(inbox_a[...])
    mine = inbox_b.at[tp, pos_b]
    finish(
        exchange(
            [
                (mine, mine, shifted(along_b(j), d))
                for j in (4, 3, 5, 2, 6, 1, 7, 0)
                for d in (2, 1, 3, 0)
                if j or d
            ],
            1,
        )
    )
    full_top, full_sums = joined(inbox_b[...].reshape(TP * RING, 2, 128))
    row_id = lax.broadcasted_iota(jnp.int32, (GROUP, 128), 0)
    row_lane = lax.broadcasted_iota(jnp.int32, (GROUP, 128), 1)

    def member(value, n):
        return jnp.sum(jnp.where(row_lane == row_id + n * GROUP, value, 0.0), axis=1, keepdims=True)

    full_total = member(full_sums, 0)
    log_norm = member(full_top, 0) + jnp.log(full_total)
    logprob = member(full_sums, 2) - log_norm
    entropy = log_norm - member(full_sums, 1) / full_total
    row_code = member(full_sums, 3).astype(jnp.int32)
    part = jnp.sum(jnp.where(row_code == row_lane + 1, logprob, 0.0), axis=0, keepdims=True)

    parts[core, pos_a] = part
    own_sum = parts.at[core, pos_a]
    copies = exchange(
        [
            (own_sum, own_sum, other)
            for p in range(RING - 1, 0, -1)
            for other in (along_a(ORDER[p]), across(along_a(ORDER[p])))
        ]
        + [(own_sum, own_sum, partner)],
        2,
    )
    row_slot = jnp.full((GROUP, 128), -1, jnp.int32)
    for r in range(ROWS):
        row_slot = jnp.where(row_lane == r, slot_of[r], row_slot)
    own_row = (row_slot >= 0) & (row_id == row_slot + pos_b * SLOTS)
    token_logprob = jnp.sum(jnp.where(own_row, logprob, 0.0), axis=0, keepdims=True)
    token_entropy = jnp.sum(jnp.where(own_row, entropy, 0.0), axis=0, keepdims=True)
    finish(copies)
    seq_logprob = jnp.sum(parts[...].reshape(2 * RING, 1, 128), axis=0)
    out_ref[0:1, :] = token_logprob
    out_ref[1:2, :] = token_entropy
    out_ref[2:3, :] = seq_logprob

    for copy in sends:
        copy.wait_send()
    everything = rows.at[pl.ds(0, RING * RING - 1)]
    remote(everything, everything, row_send, row_recv.at[0], partner).wait_send()


def split_kernel(result_ref, logprob_ref, entropy_ref, seq_ref):
    logprob_ref[...] = result_ref[0, :ROWS]
    entropy_ref[...] = result_ref[1, :ROWS]
    seq_ref[...] = result_ref[2, :SEQS]


def local(hidden, norm_gain, lm_head, targets, segments, scored):
    depth, width = lm_head.shape
    row_width = depth + 128
    smem = pl.BlockSpec(memory_space=pltpu.SMEM)
    vmem = pl.BlockSpec(memory_space=pltpu.VMEM)
    result = pl.pallas_call(
        kernel,
        out_shape=jax.ShapeDtypeStruct((8, 128), jnp.float32),
        in_specs=[smem, smem, smem, vmem, vmem, pl.BlockSpec(memory_space=pl.ANY)],
        out_specs=vmem,
        scratch_shapes=[
            pltpu.VMEM((RING * RING, SLOTS, row_width), jnp.bfloat16),
            pltpu.VMEM((2, depth, width), jnp.bfloat16),
            pltpu.VMEM((RING, 2, 128), jnp.float32),
            pltpu.VMEM((RING, 2, 128), jnp.float32),
            pltpu.VMEM((TP, RING, 2, 128), jnp.float32),
            pltpu.VMEM((2, RING, 1, 128), jnp.float32),
            pltpu.SemaphoreType.DMA,
            pltpu.SemaphoreType.DMA((RING * RING,)),
            pltpu.SemaphoreType.DMA((3,)),
            pltpu.SemaphoreType.DMA((3, TP * RING)),
            pltpu.SemaphoreType.DMA((3, TP * RING)),
        ],
        compiler_params=pltpu.CompilerParams(
            collective_id=0, has_side_effects=True, vmem_limit_bytes=56 * 1024 * 1024
        ),
    )(targets, segments, scored, hidden, norm_gain.reshape(depth // 128, 128), lm_head)
    return pl.pallas_call(
        split_kernel,
        out_shape=[jax.ShapeDtypeStruct((n,), jnp.float32) for n in (ROWS, ROWS, SEQS)],
        in_specs=[vmem],
        out_specs=[vmem, vmem, vmem],
    )(result)


def solution(mesh):
    return jax.shard_map(
        local,
        mesh=mesh,
        in_specs=(P("req", None), P(), P(None, ("req", "tp")), P("req"), P("req"), P("req")),
        out_specs=(P("req"), P("req"), P()),
        check_vma=False,
    )
```
